32 devices in a mesh: pipe: 8 (over y, x, core), dp: 4 (over z).
Axes of the slice: x: 2, y: 2, z: 4, core: 2. Of those that a mesh axis runs over, the one named last changes fastest.
Arguments:
- frames: bfloat16 [16, 512, 1280], P(None, 'dp'), may hold values from -6 to 6
- norm_gain: float32 [8, 1280], P('pipe'), may hold values from 0.25 to 1.75
- norm_shift: float32 [8, 1280], P('pipe'), may hold values from -3 to 3
- w_in: bfloat16 [8, 1280, 2560], P('pipe'), may hold values from -0.15625 to 0.15625
- b_in: float32 [8, 2560], P('pipe'), may hold values from -3 to 3
- w_out: bfloat16 [8, 2560, 1280], P('pipe'), may hold values from -0.125 to 0.125
- b_out: float32 [8, 1280], P('pipe'), may hold values from -3 to 3
- adapter_w: bfloat16 [3840, 3584], P(None, 'pipe'), may hold values from -0.09375 to 0.09375
- adapter_b: float32 [3584], P('pipe'), may hold values from -3 to 3
- frame_lengths: int32 [16, 16], replicated, may hold values from 0 to 96, as said below
- owners: int32 [16, 16], replicated, may hold values from 0 to 3, as said below
- offsets: int32 [16, 16], replicated, may hold values from 0 to 1024, as said below
Outputs:
- packed: bfloat16 [4096, 3584], P('dp', 'pipe')
The draws below stay inside these ranges and needn't reach their ends.
Inputs may be any that keep to these rules, and one draw needn't show every extreme that they name: `frame_lengths`: in every micro-batch each device's slot lengths are even and sum to 128; in every micro-batch each device has exactly one utterance slot of 96 frames. `owners`: in every micro-batch each device has exactly one slot for each owner, and every owner receives exactly 64 adapter rows of that micro-batch. `offsets`: each owner's utterances tile its 1024 rows without gaps, ordered by micro-batch and then by source device; an empty slot's offset is where it would begin.
All inputs are finite; a program needn't handle non-finite values.
Results may differ from the reference program's by a relative error of at most 0.03.
Values may be sent and summed in bfloat16 or wider, within the bound.
No kernel may reach another device: no remote copies, remote signals or barrier semaphores. Data moves between devices by JAX's collectives and lax.ppermute only.
A program may use at most 128 MiB of HBM per device.

```python
import jax
import jax.numpy as jnp
from jax import lax

D = 1280
FFN = 2560
DM = 3584
MICRO = 16
LAYERS = 8
PAIRS = 64
SLOT_MAX = 48
OWNED = 1024
ALL_FRAMES = 512
N_PIPE = 8
N_DP = 4


def packing_plan(key):
    slot_count = N_DP
    rest_rows = PAIRS - SLOT_MAX
    others = slot_count - 1
    quota_size = rest_rows // others
    extra_count = rest_rows % others
    paired_count = others // 2
    lone_count = others - 2 * paired_count

    def one_micro(micro_key):
        key_list = jax.random.split(micro_key, 5)
        base_parts = quota_size + (jnp.arange(others) >= others - extra_count).astype(jnp.int32)
        swings = jax.random.randint(key_list[0], (paired_count,), 0, quota_size + 1).astype(jnp.int32)
        swings = swings.at[0].set(quota_size)
        signed = jnp.stack([swings, -swings], axis=1).reshape(-1)
        signed = jnp.concatenate([signed, jnp.zeros((lone_count,), jnp.int32)])
        part_sizes = jnp.concatenate([jnp.full((1,), SLOT_MAX, jnp.int32), (base_parts + signed).astype(jnp.int32)])
        part_sizes = part_sizes[jax.random.permutation(key_list[1], slot_count).astype(jnp.int32)]
        owner_order = jax.random.permutation(key_list[2], slot_count).astype(jnp.int32)
        device_turn = jax.random.permutation(key_list[3], slot_count).astype(jnp.int32)

        def one_device(device_key, device_id):
            slot_order = jax.random.permutation(device_key, slot_count).astype(jnp.int32)
            slot_sizes = part_sizes[slot_order]
            slot_owner = owner_order[(slot_order + device_turn[device_id]) % slot_count]
            return (slot_sizes, slot_owner)
        device_keys = jax.random.split(key_list[4], slot_count)
        sizes_all, owners_all = jax.vmap(one_device)(device_keys, jnp.arange(slot_count, dtype=jnp.int32))
        matches = owners_all[:, :, None] == jnp.arange(slot_count, dtype=jnp.int32)
        received = jnp.sum(jnp.where(matches, sizes_all[:, :, None], 0), axis=1).astype(jnp.int32)
        earlier = (jnp.cumsum(received, axis=0) - received).astype(jnp.int32)
        offsets_all = jnp.take_along_axis(earlier, owners_all, axis=1)
        return (sizes_all, owners_all, offsets_all)
    micro_keys = jax.random.split(key, MICRO)
    sizes_all, owners_all, offsets_all = jax.vmap(one_micro)(micro_keys)
    offsets_all = offsets_all + (jnp.arange(MICRO, dtype=jnp.int32) * PAIRS)[:, None, None]
    shape_out = (MICRO, N_DP * N_DP)
    return ((2 * sizes_all).reshape(shape_out).astype(jnp.int32), owners_all.reshape(shape_out).astype(jnp.int32), offsets_all.reshape(shape_out).astype(jnp.int32))


def draw_frame_lengths(key, part):
    return packing_plan(jax.random.fold_in(key, 7))[0]


def draw_owners(key, part):
    return packing_plan(jax.random.fold_in(key, 7))[1]


def draw_offsets(key, part):
    return packing_plan(jax.random.fold_in(key, 7))[2]


def steps_of(key, shape, cuts, low, largest):
    loudness = 1.0
    for dim, parts in cuts:
        draws = jax.random.uniform(jax.random.fold_in(jax.random.fold_in(key, 6), dim), (parts,), jnp.float32, low / len(cuts), largest / len(cuts))
        loudness = loudness * jnp.repeat(jnp.exp(draws), shape[dim] // parts).reshape((-1,) + (1,) * (len(shape) - 1 - dim))
    return loudness


def bell_draw(rng, dims, deviation, bound, shards=(), kind=jnp.bfloat16):
    result = deviation * jax.random.normal(rng, dims, jnp.float32)
    if shards:
        result = result * steps_of(rng, dims, shards, -0.22, 0.18)
    return jnp.clip(result, -bound, bound).astype(kind)


def setup_inputs(seed: int = 0) -> dict:
    streams_of = jax.random.split(jax.random.key(seed), 13)
    frames = bell_draw(streams_of[0], (MICRO, ALL_FRAMES, D), 1.0, 6.0, ((1, 4),))
    norm_gain = jnp.clip(1.0 + 0.15 * jax.random.normal(streams_of[1], (LAYERS, D), jnp.float32), 0.25, 1.75)
    norm_shift = bell_draw(streams_of[2], (LAYERS, D), 0.5, 3.0, ((0, 8),), jnp.float32)
    w_in = bell_draw(streams_of[3], (LAYERS, D, FFN), D ** -0.5, 0.15625, ((0, 8),))
    b_in = bell_draw(streams_of[4], (LAYERS, FFN), 0.5, 3.0, ((0, 8),), jnp.float32)
    w_out = bell_draw(streams_of[5], (LAYERS, FFN, D), FFN ** -0.5, 0.125, ((0, 8),))
    b_out = bell_draw(streams_of[6], (LAYERS, D), 0.5, 3.0, ((0, 8),), jnp.float32)
    adapter_w = bell_draw(streams_of[7], (3 * D, DM), (3 * D) ** -0.5, 0.09375, ((1, 8),))
    adapter_b = bell_draw(streams_of[8], (DM,), 0.5, 3.0, ((0, 8),), jnp.float32)
    frame_lengths = draw_frame_lengths(jax.random.fold_in(streams_of[12], 71), 0)
    owners = draw_owners(jax.random.fold_in(streams_of[12], 71), 0)
    offsets = draw_offsets(jax.random.fold_in(streams_of[12], 71), 0)
    return {"frames": frames, "norm_gain": norm_gain, "norm_shift": norm_shift, "w_in": w_in, "b_in": b_in, "w_out": w_out, "b_out": b_out, "adapter_w": adapter_w, "adapter_b": adapter_b, "frame_lengths": frame_lengths, "owners": owners, "offsets": offsets}


def layer_norm(values, gain, shift):
    mean_value = lax.optimization_barrier(jnp.mean(values, axis=-1, keepdims=True))
    centered = values - mean_value
    variance = lax.optimization_barrier(jnp.mean(centered * centered, axis=-1, keepdims=True))
    return centered * lax.rsqrt(variance + 1e-05) * gain + shift

def encoder_layer(states, gain, shift, first_w, first_b, second_w, second_b):
    values = states.astype(jnp.float32)
    normed = layer_norm(values, gain, shift).astype(jnp.bfloat16)
    hidden_units = jnp.dot(normed, first_w, preferred_element_type=jnp.float32) + first_b
    hidden_units = jax.nn.gelu(hidden_units, approximate=False).astype(jnp.bfloat16)
    summed = values + jnp.dot(hidden_units, second_w, preferred_element_type=jnp.float32) + second_b
    return summed.astype(jnp.bfloat16)

def reference(frames, norm_gain, norm_shift, w_in, b_in, w_out, b_out, adapter_w, adapter_b, frame_lengths, owners, offsets):

    def encode(micro_block):
        states = micro_block
        for section_id in range(N_PIPE):
            states = encoder_layer(states, norm_gain[section_id], norm_shift[section_id], w_in[section_id], b_in[section_id], w_out[section_id], b_out[section_id])
        return states
    encoded = lax.map(encode, frames)
    lengths = (frame_lengths // 2).reshape(MICRO, N_DP, N_DP)
    owners_all = owners.reshape(MICRO, N_DP, N_DP)
    offsets_all = offsets.reshape(MICRO, N_DP, N_DP)
    starts = jnp.cumsum(lengths, axis=-1) - lengths
    position = jnp.arange(PAIRS, dtype=jnp.int32)
    paired = encoded.reshape(MICRO, N_DP, PAIRS, 2 * D)
    first_row = jnp.any((starts[..., None] == position) & (lengths[..., None] > 0), axis=2)
    previous = jnp.concatenate([jnp.zeros_like(paired[:, :, :1, D:]), paired[:, :, :-1, D:]], axis=2)
    previous = jnp.where(first_row[..., None], jnp.zeros_like(previous), previous)
    stacked = jnp.concatenate([previous, paired], axis=-1).reshape(-1, 3 * D)
    adapted = (jnp.dot(stacked, adapter_w, preferred_element_type=jnp.float32) + adapter_b).astype(jnp.bfloat16)
    slot_ends = starts + lengths
    slot_of = lax.optimization_barrier(jnp.sum((slot_ends[..., None] <= position).astype(jnp.int32), axis=2)).astype(jnp.int32)
    within_slot = position - jnp.take_along_axis(starts, slot_of, axis=2)
    owner_of = jnp.take_along_axis(owners_all, slot_of, axis=2)
    base_offset = jnp.take_along_axis(offsets_all, slot_of, axis=2)
    destination = (owner_of * OWNED + base_offset + within_slot).astype(jnp.int32)
    packed = jnp.zeros((N_DP * OWNED, DM), jnp.bfloat16)
    return packed.at[destination.reshape(-1)].set(adapted)
```

```python
import jax
import jax.numpy as jnp
from jax import lax
from jax.experimental import pallas as pl
from jax.experimental.pallas import tpu as pltpu
from jax.sharding import PartitionSpec as P

HOP_TICKS = 2
GROUPS = (6, 5, 3, 2)
FFN_PARTS = 2


def in_vmem(value):
    return pltpu.with_memory_space_constraint(value, pltpu.VMEM)


def vmem_spec():
    return pl.BlockSpec(memory_space=pltpu.VMEM)


def smem_spec():
    return pl.BlockSpec(memory_space=pltpu.SMEM)


def layer_norm(values, gain, shift):
    mean_value = jnp.mean(values, axis=-1, keepdims=True)
    centered = values - mean_value
    variance = jnp.mean(centered * centered, axis=-1, keepdims=True)
    return centered * lax.rsqrt(variance + 1e-05) * gain + shift


def exact_gelu(values):
    return 0.5 * values * (1.0 + lax.erf(values * 0.7071067811865476))


def layer_tick(tick, section, micro_count, fresh, inbox, params):
    rows, width = inbox.shape
    hidden = params[2].shape[1]
    part = hidden // FFN_PARTS

    def body(section_ref, fresh_ref, inbox_ref, gain, shift, first_w, first_b, second_w, second_b, out_ref, normed, total):
        place = section_ref[0]
        own_turn = tick - HOP_TICKS * place

        @pl.when(jnp.logical_and(own_turn >= 0, own_turn < micro_count))
        def _():
            values = jnp.where(place == 0, fresh_ref[...], inbox_ref[...]).astype(jnp.float32)
            normed[...] = layer_norm(values, gain[...], shift[...]).astype(jnp.bfloat16)
            total[...] = values + second_b[...]
            for index in range(FFN_PARTS):
                span = pl.ds(index * part, part)
                units = jnp.dot(normed[...], first_w[:, span], preferred_element_type=jnp.float32)
                units = exact_gelu(units + first_b[:, span]).astype(jnp.bfloat16)
                total[...] += jnp.dot(units, second_w[span, :], preferred_element_type=jnp.float32)
            out_ref[...] = total[...].astype(jnp.bfloat16)

    return pl.pallas_call(
        body,
        out_shape=jax.ShapeDtypeStruct((rows, width), jnp.bfloat16),
        in_specs=[smem_spec()] + [vmem_spec()] * 8,
        out_specs=vmem_spec(),
        scratch_shapes=[pltpu.VMEM((rows, width), jnp.bfloat16), pltpu.VMEM((rows, width), jnp.float32)],
        compiler_params=pltpu.CompilerParams(vmem_limit_bytes=12 << 20),
        name="layer_tick",
    )(section, fresh, inbox, *params)


def adapt_rows(first_micro, place, lengths, held, relayed, adapter_w, adapter_b):
    count, rows, width = held.shape
    pairs = rows // 2
    columns = adapter_w.shape[1]

    def body(place_ref, lengths_ref, held_ref, relayed_ref, weight, bias, out_ref, stacked):
        from_relay = place_ref[0]
        device = place_ref[1]
        slots = place_ref[2]
        row_ids = lax.broadcasted_iota(jnp.int32, (pairs, rows), 0)
        frame_ids = lax.broadcasted_iota(jnp.int32, (pairs, rows), 1)
        for item in range(count):
            block = jnp.where(from_relay == 1, relayed_ref[item], held_ref[item])
            is_first = row_ids < 0
            start = jnp.int32(0)
            for slot in range(SLOTS[0]):
                size = lengths_ref[first_micro + item, device * slots + slot] // 2
                is_first = jnp.logical_or(is_first, jnp.logical_and(row_ids == start, size > 0))
                start = start + size
            for tap in range(3):
                pick = frame_ids == 2 * row_ids + (tap - 1)
                if tap == 0:
                    pick = jnp.logical_and(pick, jnp.logical_not(is_first))
                pick = jnp.where(pick, 1.0, 0.0).astype(jnp.bfloat16)
                taken = jnp.dot(pick, block, preferred_element_type=jnp.float32).astype(jnp.bfloat16)
                stacked[item * pairs : (item + 1) * pairs, tap * width : (tap + 1) * width] = taken
        mixed = jnp.dot(stacked[...], weight[...], preferred_element_type=jnp.float32) + bias[...]
        out_ref[...] = mixed.astype(jnp.bfloat16)

    return pl.pallas_call(
        body,
        out_shape=jax.ShapeDtypeStruct((count * pairs, columns), jnp.bfloat16),
        in_specs=[smem_spec(), smem_spec()] + [vmem_spec()] * 4,
        out_specs=vmem_spec(),
        scratch_shapes=[pltpu.VMEM((count * pairs, 3 * width), jnp.bfloat16)],
        compiler_params=pltpu.CompilerParams(vmem_limit_bytes=24 << 20),
        name="adapt_rows",
    )(place, lengths, held, relayed, adapter_w, adapter_b)


def place_rows(first_micro, count, place, tables, blocks):
    pairs = blocks[0].shape[0] // count
    columns = blocks[0].shape[1]
    devices = len(blocks)

    def body(place_ref, lengths_ref, owners_ref, offsets_ref, *refs):
        out_ref = refs[-1]
        device = place_ref[1]
        slots = place_ref[2]
        target = lax.broadcasted_iota(jnp.int32, (pairs, pairs), 0)
        source = lax.broadcasted_iota(jnp.int32, (pairs, pairs), 1)
        for item in range(count):
            micro = first_micro + item
            span = slice(item * pairs, (item + 1) * pairs)
            total = jnp.zeros((pairs, columns), jnp.float32)
            for shift in range(devices):
                sender = (device + (devices - shift)) % devices
                start = jnp.int32(0)
                begin = jnp.int32(0)
                size = jnp.int32(0)
                onset = jnp.int32(0)
                for slot in range(devices):
                    at = sender * slots + slot
                    own = owners_ref[micro, at] == device
                    length = lengths_ref[micro, at] // 2
                    begin = jnp.where(own, start, begin)
                    size = jnp.where(own, length, size)
                    onset = jnp.where(own, offsets_ref[micro, at] - micro * pairs, onset)
                    start = start + length
                pick = jnp.logical_and(source - begin == target - onset, jnp.logical_and(source >= begin, source < begin + size))
                pick = jnp.where(pick, 1.0, 0.0).astype(jnp.bfloat16)
                total = total + jnp.dot(pick, refs[shift][span, :], preferred_element_type=jnp.float32)
            out_ref[span, :] = total.astype(jnp.bfloat16)

    return pl.pallas_call(
        body,
        out_shape=jax.ShapeDtypeStruct((count * pairs, columns), jnp.bfloat16),
        in_specs=[smem_spec()] * 4 + [vmem_spec()] * devices,
        out_specs=vmem_spec(),
        compiler_params=pltpu.CompilerParams(vmem_limit_bytes=12 << 20),
        name="place_rows",
    )(place, *tables, *blocks)


SLOTS = [0]


def relay_bits(sections):
    bits = [1 << i for i in range(sections.bit_length() - 1)]
    return bits[1:] + bits[:1]


def on_device(frames, norm_gain, norm_shift, w_in, b_in, w_out, b_out, adapter_w, adapter_b, frame_lengths, owners, offsets):
    sections = lax.axis_size("pipe")
    section_id = lax.axis_index("pipe")
    devices = lax.axis_size("dp")
    device_id = lax.axis_index("dp")
    micro_count, frame_rows, width = frames.shape
    SLOTS[0] = devices
    section = section_id.astype(jnp.int32).reshape(1)
    params = (norm_gain, norm_shift, in_vmem(w_in[0]), b_in, in_vmem(w_out[0]), b_out)
    forward = [(i, i + 1) for i in range(sections - 1)]
    last_tick = micro_count + HOP_TICKS * (sections - 1)
    ready = {}
    at = 0
    for size in GROUPS:
        ready[at + size - 1 + HOP_TICKS * (sections - 1)] = (at, size)
        at += size
    bias = adapter_b.reshape(1, -1)
    from_relay = (section_id % 2 == 0).astype(jnp.int32)
    place = jnp.stack([from_relay, device_id.astype(jnp.int32), jnp.int32(devices)])
    tables = (frame_lengths, owners, offsets)

    def finish(first, count, held):
        bits = relay_bits(sections)
        holders = [sections - 1]
        relayed = held
        for bit in bits:
            relayed = lax.ppermute(held, "pipe", [(h, h ^ bit) for h in holders])
            if bit != bits[-1]:
                fresh = section_id == holders[0] ^ bit
                for h in holders[1:]:
                    fresh = jnp.logical_or(fresh, section_id == h ^ bit)
                held = jnp.where(fresh, relayed, held)
            holders = holders + [h ^ bit for h in holders]
        own = adapt_rows(first, place, frame_lengths, held, relayed, adapter_w, bias)
        blocks = [own]
        for shift in range(1, devices):
            blocks.append(lax.ppermute(own, "dp", [(i, (i + shift) % devices) for i in range(devices)]))
        return place_rows(first, count, place, tables, blocks)

    inboxes = {}
    results = []
    pieces = []
    for tick in range(last_tick):
        fresh = frames[min(tick, micro_count - 1)]
        inbox = inboxes.pop(tick, None)
        if inbox is None:
            inbox = fresh
        result = layer_tick(tick, section, micro_count, fresh, inbox, params)
        if tick + HOP_TICKS < last_tick:
            inboxes[tick + HOP_TICKS] = lax.ppermute(result, "pipe", forward)
        if tick >= HOP_TICKS * (sections - 1):
            results.append(result)
        if tick in ready:
            first, count = ready[tick]
            pieces.append(finish(first, count, jnp.stack(results)))
            results = []
    return jnp.concatenate(pieces, axis=0)


def solution(mesh):
    placed = (
        P(None, "dp", None),
        P("pipe", None),
        P("pipe", None),
        P("pipe", None, None),
        P("pipe", None),
        P("pipe", None, None),
        P("pipe", None),
        P(None, "pipe"),
        P("pipe"),
        P(),
        P(),
        P(),
    )
    return jax.shard_map(on_device, mesh=mesh, in_specs=placed, out_specs=P("dp", "pipe"), check_vma=False)
```
